32 devices in a mesh: expert: 32 (over z, y, x, core).
Axes of the slice: x: 2, y: 2, z: 4, core: 2. Of those that a mesh axis runs over, the one named last changes fastest.
Arguments:
- tokens: bfloat16 [6144, 2048], P('expert'), may hold values from -6 to 6
- seg_ids: int32 [32, 192], P('expert'), may hold values from 0 to 11, never falling along the last dimension, each value on 1 to 128 neighbouring positions
- routes: int32 [6144, 8], P('expert'), may hold values from 0 to 31, all different within a row; in each aligned block of 192 rows (0 to 191, 192 to 383, ...) at most 60 rows name the same one
- attn_gain: bfloat16 [2048], P('expert'), may hold values from 0.5 to 1.5
- w_query: bfloat16 [2048, 4096], P('expert'), may hold values from -0.125 to 0.125
- key_projection_weight: bfloat16 [2048, 512], P('expert'), may hold values from -0.125 to 0.125
- value_projection_weight: bfloat16 [2048, 512], P('expert'), may hold values from -0.125 to 0.125
- w_out: bfloat16 [4096, 2048], P('expert'), may hold values from -0.25 to 0.25
- query_key_gains: float32 [2, 128], replicated, may hold values from 0.1 to 1.9
- ffn_gain: bfloat16 [2048], P('expert'), may hold values from 0.5 to 1.5
- w_router: bfloat16 [2048, 32], P('expert'), may hold values from -0.125 to 0.125
- w_gate: bfloat16 [32, 2048, 768], P('expert'), may hold values from -0.125 to 0.125
- w_up: bfloat16 [32, 2048, 768], P('expert'), may hold values from -0.125 to 0.125
- w_down: bfloat16 [32, 768, 2048], P('expert'), may hold values from -0.4375 to 0.4375
- cotangent: float32 [6144, 2048], P('expert'), may hold values from -6 to 6
Outputs:
- block_out: bfloat16 [6144, 2048], P('expert')
- grad_tokens: float32 [6144, 2048], P('expert')
- grad_attn_gain: float32 [2048], P('expert')
- grad_query: float32 [2048, 4096], P('expert')
- grad_key: float32 [2048, 512], P('expert')
- grad_value: float32 [2048, 512], P('expert')
- grad_out: float32 [4096, 2048], P('expert')
- grad_qk_gains: float32 [2, 128], replicated
- grad_ffn_gain: float32 [2048], P('expert')
- grad_router: float32 [2048, 32], P('expert')
- grad_gate: float32 [32, 2048, 768], P('expert')
- grad_up: float32 [32, 2048, 768], P('expert')
- grad_down: float32 [32, 768, 2048], P('expert')
The draws below stay inside these ranges and needn't reach their ends.
Inputs may be any that keep to these rules, and one draw needn't show every extreme that they name: `routes`: the 8 experts of a token differ. Among the 192 tokens of one device no expert is chosen more than 60 times, and in every draw some device chooses some expert exactly 60 times. `seg_ids`: along a row the numbers never fall; a sequence has 1 to 128 tokens and some sequence has exactly 128.
All inputs are finite; a program needn't handle non-finite values.
Results may differ from the reference program's by a relative error of at most 0.015.
Values may be sent and summed in bfloat16 or wider, within the bound.
No kernel may reach another device: no remote copies, remote signals or barrier semaphores. Data moves between devices by JAX's collectives and lax.ppermute only.
A program may use at most 384 MiB of HBM per device.

```python
import math
import jax
import jax.numpy as jnp
import numpy as np
from jax import lax

MODEL_DIM = 2048
QUERY_HEADS = 32
KEY_VALUE_HEADS = 4
HEAD_WIDTH = 128
FF = 768
TOPK = 8
TOK_DEV = 192
SEQ_MAX = 128
EXPERTS = 32
SHARDS = 32
TOKENS = 6144
CAP = 60


def block_levels(key, dims, cuts, least, high):
    loudness, own = 1.0, jax.random.fold_in(key, 6)
    for dim, shards_of in cuts:
        steps = jnp.exp(jax.random.uniform(jax.random.fold_in(own, dim), (shards_of,), jnp.float32, least / len(cuts), high / len(cuts)))
        loudness = loudness * jnp.repeat(steps, dims[dim] // shards_of).reshape([-1 if axis == dim else 1 for axis in range(len(dims))])
    return loudness


def profile(amount, total, bound, skew):
    portions = [(1 << 20) // math.isqrt(standing ** skew) + 1 for standing in range(2, amount + 1)]
    rest, counts = total - bound - (amount - 1), [1] * (amount - 1)
    while rest > 0:
        free = [i for i in range(amount - 1) if counts[i] < bound]
        mass, budget = sum([portions[i] for i in free]), rest
        for i in free:
            more = min(bound - counts[i], max(1, budget * portions[i] // mass), rest)
            counts[i] = counts[i] + more
            rest = rest - more
    return np.array([bound] + counts)


def ragged(own_key, amount, total, bound, skew):
    if amount == 2:
        one = jax.random.randint(own_key, (), max(1, total - bound), min(bound, total - 1) + 1)
        return jnp.stack([one, total - one])
    tallies = jnp.asarray(profile(amount, total, bound, skew), jnp.int32)
    pairs = (amount - 1) // 2
    donor, sink = tallies[1:1 + 2 * pairs:2], tallies[2:2 + 2 * pairs:2]
    room = jnp.minimum(donor - 1, bound - sink)
    moved = jax.random.randint(jax.random.fold_in(own_key, 1), (pairs,), 0, 1 << 20) % (room + 1)
    tallies = tallies.at[1:1 + 2 * pairs:2].set(donor - moved).at[2:2 + 2 * pairs:2].set(sink + moved)
    return tallies[jax.random.permutation(jax.random.fold_in(own_key, 2), amount)]


def assign_block(rng, own, number, rows, amount, top, most, skew):
    order = jax.random.permutation(rng, amount)
    heavy_load, common = load_shares(amount, rows * top, most, skew, True), load_shares(amount, rows * top, most, skew, False)
    places = jnp.arange(amount)

    def named(lengths, turn):
        used = int((lengths > 0).sum())
        fixed = max(1, used // 4)
        passed = fixed + (places - fixed + turn * (used - fixed)) % max(1, amount - fixed)
        return jnp.zeros((amount,), jnp.int32).at[order[jnp.where(places < fixed, places, passed)]].set(jnp.asarray(lengths, jnp.int32))

    lengths = jnp.where(number % 4 == 0, named(heavy_load, number // 4), named(common, number - number // 4 - 1))
    mixed = jax.random.permutation(jax.random.fold_in(own, 3), amount)
    giver, sink = mixed[0:amount // 2 * 2:2], mixed[1:amount // 2 * 2:2]
    margin = jnp.minimum(lengths[giver] - 1, most - lengths[sink]) // 2
    margin = jnp.where((giver == order[0]) | (sink == order[0]) | (lengths[sink] == 0), 0, jnp.maximum(margin, 0))
    passed = jax.random.randint(jax.random.fold_in(own, 4), (amount // 2,), 0, 1 << 20) % (margin + 1)
    lengths = lengths.at[giver].add(-passed).at[sink].add(passed)
    labels = jnp.searchsorted(jnp.cumsum(lengths), jnp.arange(rows * top), side="right").astype(jnp.int32)
    grid = labels.reshape(top, rows).T
    grid = grid[jax.random.permutation(jax.random.fold_in(own, 1), rows)]
    turn = jax.random.randint(jax.random.fold_in(own, 2), (rows, 1), 0, top)
    return jnp.take_along_axis(grid, (jnp.arange(top)[None, :] + turn) % top, axis=1)


def load_shares(amount, total, reach, skew, full):
    weights = [(1 << 20) // math.isqrt(standing ** skew) + 1 for standing in range(1, amount + 1)]
    largest = reach if full else min(reach, max(-(-total // amount), total * weights[0] // sum(weights)))
    least = 1 if total - largest >= amount - 1 else 0
    holding, spare = [largest] + [least] * (amount - 1), total - largest - least * (amount - 1)
    while spare > 0:
        candidates = [i for i in range(1, amount) if holding[i] < largest] or [i for i in range(1, amount) if holding[i] < reach]
        pool, left = sum([weights[i] for i in candidates]), spare
        for i in candidates:
            more = min(reach - holding[i], max(1, left * weights[i] // pool), spare)
            holding[i] = holding[i] + more
            spare = spare - more
    return np.array(holding)


def gaussian(rng, dims, scale, most, cuts=(), held_as=jnp.bfloat16):
    values = scale * jax.random.normal(rng, dims, jnp.float32)
    if cuts:
        values = values * block_levels(rng, dims, cuts, -0.22, 0.18)
    return jnp.clip(values, -most, most).astype(held_as)


def setup_inputs(seed: int = 0) -> dict:
    seeds = jax.random.split(jax.random.key(seed), 16)
    tokens = gaussian(seeds[0], (TOKENS, MODEL_DIM), 1.0, 6.0, ((0, 32),))
    seg_ids = jax.vmap(lambda own: jnp.searchsorted(jnp.cumsum(ragged(own, TOK_DEV // 16, TOK_DEV, SEQ_MAX, 1)), jnp.arange(TOK_DEV), side="right"))(jax.random.split(seeds[1], SHARDS)).reshape((SHARDS, TOK_DEV)).astype(jnp.int32)
    routes_keys = jax.random.split(jax.random.fold_in(seeds[2], 1), TOKENS // TOK_DEV)
    routes_turns = jax.random.permutation(jax.random.fold_in(seeds[2], 3), TOKENS // TOK_DEV)
    routes = jax.vmap(lambda own, number: assign_block(jax.random.fold_in(seeds[2], 2), own, number, TOK_DEV, EXPERTS, TOPK, CAP, 1))(routes_keys, routes_turns).reshape((TOKENS, TOPK))
    attn_gain = jnp.clip(1.0 + 0.1 * jax.random.normal(seeds[3], (MODEL_DIM,), jnp.float32), 0.5, 1.5).astype(jnp.bfloat16)
    w_query = gaussian(seeds[4], (MODEL_DIM, QUERY_HEADS * HEAD_WIDTH), MODEL_DIM ** -0.5, 0.125, ((0, 32),))
    key_projection_weight = gaussian(seeds[5], (MODEL_DIM, KEY_VALUE_HEADS * HEAD_WIDTH), MODEL_DIM ** -0.5, 0.125, ((0, 32),))
    value_projection_weight = gaussian(seeds[6], (MODEL_DIM, KEY_VALUE_HEADS * HEAD_WIDTH), MODEL_DIM ** -0.5, 0.125, ((0, 32),))
    w_out = gaussian(seeds[7], (QUERY_HEADS * HEAD_WIDTH, MODEL_DIM), (QUERY_HEADS * HEAD_WIDTH // 8) ** -0.5, 0.25, ((0, 32),))
    query_key_gains = jnp.clip(1.0 + 0.18 * jax.random.normal(seeds[8], (2, HEAD_WIDTH), jnp.float32), 0.1, 1.9)
    ffn_gain = jnp.clip(1.0 + 0.1 * jax.random.normal(seeds[9], (MODEL_DIM,), jnp.float32), 0.5, 1.5).astype(jnp.bfloat16)
    w_router = gaussian(seeds[10], (MODEL_DIM, EXPERTS), MODEL_DIM ** -0.5, 0.125, ((0, 32),))
    w_gate = gaussian(seeds[11], (EXPERTS, MODEL_DIM, FF), MODEL_DIM ** -0.5, 0.125, ((0, 32),))
    w_up = gaussian(seeds[12], (EXPERTS, MODEL_DIM, FF), MODEL_DIM ** -0.5, 0.125, ((0, 32),))
    w_down = gaussian(seeds[13], (EXPERTS, FF, MODEL_DIM), (FF // 4) ** -0.5, 0.4375, ((0, 32),))
    cotangent = gaussian(seeds[14], (TOKENS, MODEL_DIM), 1.0, 6.0, ((0, 32),), jnp.float32)
    return {"tokens": tokens, "seg_ids": seg_ids, "routes": routes, "attn_gain": attn_gain, "w_query": w_query, "key_projection_weight": key_projection_weight, "value_projection_weight": value_projection_weight, "w_out": w_out, "query_key_gains": query_key_gains, "ffn_gain": ffn_gain, "w_router": w_router, "w_gate": w_gate, "w_up": w_up, "w_down": w_down, "cotangent": cotangent}


NORM_EPSILON = 1e-06
ROPE_THETA = 1000000.0
MASK_FLOOR = 1e+30

def norm_rows(values, gain_vector):
    factor = lax.rsqrt(lax.optimization_barrier(jnp.mean(values * values, axis=-1, keepdims=True)) + NORM_EPSILON)
    unit_rows = values * factor
    return (unit_rows * gain_vector, unit_rows, factor)

def norm_gradient_rows(gradient, unit_rows, factor, gain_vector):
    scaled = gradient * gain_vector
    return factor * (scaled - unit_rows * lax.optimization_barrier(jnp.mean(scaled * unit_rows, axis=-1, keepdims=True)))

def apply_rotary(values, cosine_lookup, sine_lookup):
    half_size = values.shape[-1] // 2
    first_half = values[..., :half_size]
    second_half = values[..., half_size:]
    cos_wide = cosine_lookup[:, None, :]
    sin_wide = sine_lookup[:, None, :]
    return jnp.concatenate([first_half * cos_wide - second_half * sin_wide, second_half * cos_wide + first_half * sin_wide], axis=-1)

def layout(segment):
    row_count = segment.shape[0]
    row_index = jnp.arange(row_count, dtype=jnp.int32)
    same_seq = segment[:, None] == segment[None, :]
    positions = lax.optimization_barrier(jnp.sum(jnp.where(same_seq & (row_index[None, :] < row_index[:, None]), 1, 0), axis=1)).astype(jnp.int32)
    allowed = same_seq & (row_index[None, :] <= row_index[:, None])
    half_size = HEAD_WIDTH // 2
    inverse_freq = ROPE_THETA ** (-jnp.arange(half_size, dtype=jnp.float32) / half_size)
    angles = positions.astype(jnp.float32)[:, None] * inverse_freq[None, :]
    return (allowed, jnp.cos(angles), jnp.sin(angles))

def elementwise_product(pattern, left_side, right_side):
    return jnp.einsum(pattern, left_side.astype(jnp.float32), right_side.astype(jnp.float32))

def attention_forward(block_rows, segment, weight_set):
    gain_first, query_weight, key_matrix, value_matrix, out_weight, query_key_gains = weight_set
    token_count = block_rows.shape[0]
    heads_per_group = QUERY_HEADS // KEY_VALUE_HEADS
    score_scale = 1.0 / math.sqrt(HEAD_WIDTH)
    allowed, cosine_lookup, sine_lookup = layout(segment)
    tokens_wide = block_rows.astype(jnp.float32)
    normed_first, unit_first, factor_first = norm_rows(tokens_wide, gain_first.astype(jnp.float32))
    rows_after_norm = normed_first.astype(jnp.bfloat16)
    query_proj = jnp.dot(rows_after_norm, query_weight, preferred_element_type=jnp.float32).reshape(token_count, QUERY_HEADS, HEAD_WIDTH)
    key_projected = jnp.dot(rows_after_norm, key_matrix, preferred_element_type=jnp.float32).reshape(token_count, KEY_VALUE_HEADS, HEAD_WIDTH)
    value_projected = jnp.dot(rows_after_norm, value_matrix, preferred_element_type=jnp.float32).astype(jnp.bfloat16).reshape(token_count, KEY_VALUE_HEADS, HEAD_WIDTH)
    query_after_norm, query_unit, query_factor = norm_rows(query_proj, query_key_gains[0])
    key_normed, key_unit_rows, key_inverse_norm = norm_rows(key_projected, query_key_gains[1])
    query_rotated = apply_rotary(query_after_norm, cosine_lookup, sine_lookup).astype(jnp.bfloat16).reshape(token_count, KEY_VALUE_HEADS, heads_per_group, HEAD_WIDTH)
    key_rot = apply_rotary(key_normed, cosine_lookup, sine_lookup).astype(jnp.bfloat16)
    scores = elementwise_product('tngd,snd->ngts', query_rotated, key_rot) * score_scale
    masked = jnp.where(allowed, scores, -MASK_FLOOR)
    row_top = lax.optimization_barrier(jnp.max(masked, axis=-1, keepdims=True))
    weights_raw = jnp.where(allowed, jnp.exp(masked - row_top), 0.0)
    row_total = lax.optimization_barrier(jnp.sum(weights_raw, axis=-1, keepdims=True))
    log_total = row_top + jnp.log(row_total)
    attn_probs = (weights_raw / row_total).astype(jnp.bfloat16)
    head_out = elementwise_product('ngts,snd->tngd', attn_probs, value_projected).astype(jnp.bfloat16)
    residual_mid = tokens_wide + jnp.dot(head_out.reshape(token_count, QUERY_HEADS * HEAD_WIDTH), out_weight, preferred_element_type=jnp.float32)
    kept = (allowed, cosine_lookup, sine_lookup, rows_after_norm, unit_first, factor_first, value_projected, query_unit, query_factor, key_unit_rows, key_inverse_norm, query_rotated, key_rot, log_total, head_out)
    return (residual_mid, kept)

def attention_backward(block_rows, segment, weight_set, grad_mid):
    gain_first, query_weight, key_matrix, value_matrix, out_weight, query_key_gains = weight_set
    token_count = block_rows.shape[0]
    score_scale = 1.0 / math.sqrt(HEAD_WIDTH)
    residual_mid, kept = attention_forward(block_rows, segment, weight_set)
    allowed, cosine_lookup, sine_lookup, rows_after_norm, unit_first, factor_first, value_projected, query_unit, query_factor, key_unit_rows, key_inverse_norm, query_rotated, key_rot, log_total, head_out = kept
    grad_attn = grad_mid.astype(jnp.bfloat16)
    flat_heads = head_out.reshape(token_count, QUERY_HEADS * HEAD_WIDTH)
    out_term = jnp.dot(flat_heads.T, grad_attn, preferred_element_type=jnp.float32)
    heads_gradient = jnp.dot(grad_attn, out_weight.T, preferred_element_type=jnp.float32).astype(jnp.bfloat16).reshape(head_out.shape)
    scores = elementwise_product('tngd,snd->ngts', query_rotated, key_rot) * score_scale
    recomputed_probabilities = jnp.where(allowed, jnp.exp(jnp.where(allowed, scores, -MASK_FLOOR) - log_total), 0.0)
    grad_probs = elementwise_product('tngd,snd->ngts', heads_gradient, value_projected)
    row_delta = elementwise_product('tngd,tngd->ngt', heads_gradient, head_out)[..., None]
    grad_scores = (recomputed_probabilities * (grad_probs - row_delta)).astype(jnp.bfloat16)
    grad_qrot = (elementwise_product('ngts,snd->tngd', grad_scores, key_rot) * score_scale).reshape(token_count, QUERY_HEADS, HEAD_WIDTH)
    grad_krot = elementwise_product('qwor,oqwk->rqk', grad_scores, query_rotated) * score_scale
    value_projection_gradient = elementwise_product('qwor,oqwk->rqk', recomputed_probabilities.astype(jnp.bfloat16), heads_gradient).astype(jnp.bfloat16).reshape(token_count, KEY_VALUE_HEADS * HEAD_WIDTH)
    query_back = apply_rotary(grad_qrot, cosine_lookup, -sine_lookup)
    key_gradient_rows = apply_rotary(grad_krot, cosine_lookup, -sine_lookup)
    gain_terms = jnp.stack([lax.optimization_barrier(jnp.sum(query_back * query_unit, axis=(0, 1))), lax.optimization_barrier(jnp.sum(key_gradient_rows * key_unit_rows, axis=(0, 1)))])
    query_raw = norm_gradient_rows(query_back, query_unit, query_factor, query_key_gains[0]).astype(jnp.bfloat16).reshape(token_count, QUERY_HEADS * HEAD_WIDTH)
    key_unscaled = norm_gradient_rows(key_gradient_rows, key_unit_rows, key_inverse_norm, query_key_gains[1]).astype(jnp.bfloat16).reshape(token_count, KEY_VALUE_HEADS * HEAD_WIDTH)
    query_term = jnp.dot(rows_after_norm.T, query_raw, preferred_element_type=jnp.float32)
    key_term = jnp.dot(rows_after_norm.T, key_unscaled, preferred_element_type=jnp.float32)
    value_term = jnp.dot(rows_after_norm.T, value_projection_gradient, preferred_element_type=jnp.float32)
    grad_normed = jnp.dot(query_raw, query_weight.T, preferred_element_type=jnp.float32) + jnp.dot(key_unscaled, key_matrix.T, preferred_element_type=jnp.float32) + jnp.dot(value_projection_gradient, value_matrix.T, preferred_element_type=jnp.float32)
    first_gain_term = lax.optimization_barrier(jnp.sum(grad_normed * unit_first, axis=0))
    grad_block = grad_mid + norm_gradient_rows(grad_normed, unit_first, factor_first, gain_first.astype(jnp.float32))
    return ((first_gain_term, query_term, key_term, value_term, out_term, gain_terms), grad_block)

def reference(tokens, seg_ids, routes, attn_gain, w_query, key_projection_weight, value_projection_weight, w_out, query_key_gains, ffn_gain, w_router, w_gate, w_up, w_down, cotangent):
    shards = seg_ids.shape[0]
    token_count = seg_ids.shape[1]
    model_width_size = tokens.shape[1]
    experts = w_router.shape[1]
    top_count = routes.shape[1]
    pair_count = token_count * top_count
    all_tokens = shards * token_count
    capacity = CAP
    weight_set = (attn_gain, w_query, key_projection_weight, value_projection_weight, w_out, query_key_gains)
    blocks = tokens.reshape(shards, token_count, model_width_size)
    residual_mid = lax.map(lambda inputs: attention_forward(inputs[0], inputs[1], weight_set)[0], (blocks, seg_ids)).reshape(all_tokens, model_width_size)
    normed_second, unit_second, factor_second = norm_rows(residual_mid, ffn_gain.astype(jnp.float32))
    moe_rows = normed_second.astype(jnp.bfloat16)
    logits = jnp.dot(moe_rows, w_router, preferred_element_type=jnp.float32)
    expert_ids = jnp.arange(experts, dtype=jnp.int32)
    chosen_hot = routes[:, :, None] == expert_ids[None, None, :]
    chosen = lax.optimization_barrier(jnp.sum(jnp.where(chosen_hot, logits[:, None, :], 0.0), axis=-1))
    route_share = jax.nn.softmax(chosen, axis=-1)

    def place(route_row):
        one_hot = (route_row[:, None] == expert_ids[None, :]).astype(jnp.int32)
        slot_index = lax.optimization_barrier(jnp.sum(one_hot * jnp.cumsum(one_hot, axis=0), axis=1)) - 1
        dest_slot = (route_row * capacity + slot_index).astype(jnp.int32)
        return jnp.full((experts * capacity,), pair_count, jnp.int32).at[dest_slot].set(jnp.arange(pair_count, dtype=jnp.int32))
    source_pair = lax.map(place, routes.reshape(shards, pair_count))
    pair_base = (jnp.arange(shards, dtype=jnp.int32) * pair_count)[:, None]
    pair_table = jnp.where(source_pair < pair_count, source_pair + pair_base, all_tokens * top_count).astype(jnp.int32)
    pair_table = pair_table.reshape(shards, experts, capacity).transpose(1, 0, 2).reshape(experts, shards * capacity)
    rows_ext = jnp.concatenate([moe_rows, jnp.zeros((1, model_width_size), jnp.bfloat16)], axis=0)
    cot_ext = jnp.concatenate([cotangent, jnp.zeros((1, model_width_size), jnp.float32)], axis=0)
    share_ext = jnp.concatenate([route_share.reshape(-1), jnp.zeros((1,), jnp.float32)], axis=0)

    def expert_step(running, inputs):
        moe_sum, grad_rows_sum, grad_share = running
        pair_ids, gate_weight, up_weight, down_weight = inputs
        token_index = pair_ids // top_count
        picked_rows = rows_ext[token_index]
        gate_pre = jnp.dot(picked_rows, gate_weight, preferred_element_type=jnp.float32)
        up_pre = jnp.dot(picked_rows, up_weight, preferred_element_type=jnp.float32)
        sigmoid_gate = jax.nn.sigmoid(gate_pre)
        silu_gate = gate_pre * sigmoid_gate
        hidden = (silu_gate * up_pre).astype(jnp.bfloat16)
        result = jnp.dot(hidden, down_weight, preferred_element_type=jnp.float32).astype(jnp.bfloat16)
        pair_share = share_ext[pair_ids]
        cot_rows = cot_ext[token_index]
        moe_sum = moe_sum.at[token_index].add(pair_share[:, None] * result.astype(jnp.float32))
        grad_share = grad_share.at[pair_ids].set(lax.optimization_barrier(jnp.sum(cot_rows * result.astype(jnp.float32), axis=1)))
        grad_result = (pair_share[:, None] * cot_rows).astype(jnp.bfloat16)
        grad_hidden = jnp.dot(grad_result, down_weight.T, preferred_element_type=jnp.float32)
        down_term = jnp.dot(hidden.T, grad_result, preferred_element_type=jnp.float32)
        grad_gate_pre = (grad_hidden * up_pre * sigmoid_gate * (1.0 + gate_pre * (1.0 - sigmoid_gate))).astype(jnp.bfloat16)
        grad_up_pre = (grad_hidden * silu_gate).astype(jnp.bfloat16)
        gate_term = jnp.dot(picked_rows.T, grad_gate_pre, preferred_element_type=jnp.float32)
        up_term = jnp.dot(picked_rows.T, grad_up_pre, preferred_element_type=jnp.float32)
        grad_back = (jnp.dot(grad_gate_pre, gate_weight.T, preferred_element_type=jnp.float32) + jnp.dot(grad_up_pre, up_weight.T, preferred_element_type=jnp.float32)).astype(jnp.bfloat16)
        grad_rows_sum = grad_rows_sum.at[token_index].add(grad_back.astype(jnp.float32))
        return ((moe_sum, grad_rows_sum, grad_share), (gate_term, up_term, down_term))
    start_state = (jnp.zeros((all_tokens + 1, model_width_size), jnp.float32), jnp.zeros((all_tokens + 1, model_width_size), jnp.float32), jnp.zeros((all_tokens * top_count + 1,), jnp.float32))
    final_state, expert_grads = lax.scan(expert_step, start_state, (pair_table, w_gate, w_up, w_down))
    moe_sum = final_state[0][:all_tokens]
    block_out = (residual_mid + moe_sum).astype(jnp.bfloat16)
    grad_share = final_state[2][:all_tokens * top_count].reshape(all_tokens, top_count)
    grad_chosen = route_share * (grad_share - lax.optimization_barrier(jnp.sum(route_share * grad_share, axis=1, keepdims=True)))
    grad_logits = lax.optimization_barrier(jnp.sum(jnp.where(chosen_hot, grad_chosen[:, :, None], 0.0), axis=1)).astype(jnp.bfloat16)
    grad_router = jnp.dot(moe_rows.T, grad_logits, preferred_element_type=jnp.float32)
    grad_second = final_state[1][:all_tokens] + jnp.dot(grad_logits, w_router.T, preferred_element_type=jnp.float32)
    grad_ffn_gain = lax.optimization_barrier(jnp.sum(grad_second * unit_second, axis=0))
    grad_mid = cotangent + norm_gradient_rows(grad_second, unit_second, factor_second, ffn_gain.astype(jnp.float32))

    def attention_step(running, inputs):
        block_rows, segment, grad_block = inputs
        terms, grad_input = attention_backward(block_rows, segment, weight_set, grad_block)
        return (tuple((left_side + right_side for left_side, right_side in zip(running, terms))), grad_input)
    zeroed_terms = (jnp.zeros((model_width_size,), jnp.float32), jnp.zeros((model_width_size, QUERY_HEADS * HEAD_WIDTH), jnp.float32), jnp.zeros((model_width_size, KEY_VALUE_HEADS * HEAD_WIDTH), jnp.float32), jnp.zeros((model_width_size, KEY_VALUE_HEADS * HEAD_WIDTH), jnp.float32), jnp.zeros((QUERY_HEADS * HEAD_WIDTH, model_width_size), jnp.float32), jnp.zeros((2, HEAD_WIDTH), jnp.float32))
    sums_all, grad_tokens = lax.scan(attention_step, zeroed_terms, (blocks, seg_ids, grad_mid.reshape(shards, token_count, model_width_size)))
    return (block_out, grad_tokens.reshape(all_tokens, model_width_size), sums_all[0], sums_all[1], sums_all[2], sums_all[3], sums_all[4], sums_all[5], grad_ffn_gain, grad_router, expert_grads[0], expert_grads[1], expert_grads[2])
```

```python
import math

import jax
import jax.numpy as jnp
from jax import lax
from jax.experimental import pallas as pl
from jax.experimental.pallas import tpu as pltpu
from jax.sharding import PartitionSpec as P

NORM_EPSILON = 1e-06
ROPE_THETA = 1000000.0
MASK_FLOOR = 1e30
LANES = 128
AXIS = "expert"
F32 = jnp.float32
BF16 = jnp.bfloat16


def dot_f32(left, right):
    return jnp.dot(left, right, preferred_element_type=F32)


def dot_rows(left, right):
    return jnp.einsum("tj,ij->ti", left, right, preferred_element_type=F32)


def dot_tokens(left, right):
    return jnp.einsum("ti,tj->ij", left, right, preferred_element_type=F32)


def norm_rows(values, gain_vector):
    factor = lax.rsqrt(jnp.mean(values * values, axis=-1, keepdims=True) + NORM_EPSILON)
    unit_rows = values * factor
    return (unit_rows * gain_vector, unit_rows, factor)


def norm_gradient_rows(gradient, unit_rows, factor, gain_vector):
    scaled = gradient * gain_vector
    return factor * (scaled - unit_rows * jnp.mean(scaled * unit_rows, axis=-1, keepdims=True))


def apply_rotary(values, cosine_lookup, sine_lookup):
    half_size = values.shape[-1] // 2
    first_half = values[..., :half_size]
    second_half = values[..., half_size:]
    cos_wide = cosine_lookup[:, None, :]
    sin_wide = sine_lookup[:, None, :]
    return jnp.concatenate(
        [
            first_half * cos_wide - second_half * sin_wide,
            second_half * cos_wide + first_half * sin_wide,
        ],
        axis=-1,
    )


def layout(segment, head_size):
    row_count = segment.shape[0]
    row_index = jnp.arange(row_count, dtype=jnp.int32)
    same_seq = segment[:, None] == segment[None, :]
    positions = jnp.sum(
        jnp.where(same_seq & (row_index[None, :] < row_index[:, None]), 1, 0), axis=1
    ).astype(jnp.int32)
    allowed = same_seq & (row_index[None, :] <= row_index[:, None])
    half_size = head_size // 2
    inverse_freq = ROPE_THETA ** (-jnp.arange(half_size, dtype=F32) / half_size)
    angles = positions.astype(F32)[:, None] * inverse_freq[None, :]
    return (allowed, jnp.cos(angles), jnp.sin(angles))


class Wires:
    def __init__(self, shards):
        self.shards = shards
        self.bits = shards.bit_length() - 1
        assert shards == 1 << self.bits and self.bits >= 3
        self.far = (self.bits - 1, self.bits - 2)
        self.near = tuple(range(1, self.bits - 2))

    def swap(self, block, bit):
        return lax.ppermute(block, AXIS, [(i, i ^ (1 << bit)) for i in range(self.shards)])

    def place(self, mask):
        spot = 0
        for bit in range(self.bits):
            if bit == self.bits - 1:
                to = 0
            elif bit == self.bits - 2:
                to = 1
            elif bit == 0:
                to = self.bits - 1
            else:
                to = bit + 1
            spot = spot | (((mask >> bit) & 1) << to)
        return spot

    def to_relative(self, rows):
        order = [0] * self.shards
        for mask in range(self.shards):
            order[self.place(mask)] = mask
        return xor_blocks(rows, lax.axis_index(AXIS), order)

    def to_natural(self, rows):
        order = [self.place(block) for block in range(self.shards)]
        return xor_blocks(rows, self.place(lax.axis_index(AXIS)), order)

    def gather_small(self, shard):
        for bit in self.far + self.near + (0,):
            shard = jnp.concatenate([shard, self.swap(shard, bit)], axis=0)
        shards, bits = self.shards, self.bits
        block = shard.reshape(shards, -1)
        spots = []
        stage_of = {bit: s for s, bit in enumerate(self.far + self.near + (0,))}
        for mask in range(shards):
            spots.append(sum(((mask >> bit) & 1) << stage_of[bit] for bit in range(bits)))
        index = lax.axis_index(AXIS)
        for stage, bit in enumerate(self.far + self.near + (0,)):
            pairs = block.reshape(-1, 2, 1 << stage, block.shape[-1])
            block = jnp.where(((index >> bit) & 1) == 1, pairs[:, ::-1], pairs).reshape(block.shape)
        ordered = jnp.concatenate([block[s : s + 1] for s in spots], axis=0)
        return ordered.reshape(shard.shape)

    def gather_far(self, shard):
        for bit in self.far:
            shard = jnp.concatenate([shard, self.swap(shard, bit)], axis=0)
        return shard

    def gather_near(self, stack, split):
        halves = []
        for part, order in ((stack[:, :split], self.near), (stack[:, split:], self.near[::-1])):
            pieces = {0: part}
            for bit in order:
                for mask in list(pieces):
                    pieces[mask | (1 << bit)] = self.swap(pieces[mask], bit)
            halves.append(pieces)
        return halves

    def gather_core(self, halves):
        out = []
        for pieces in halves:
            whole = dict(pieces)
            for mask in list(pieces):
                whole[mask | 1] = self.swap(pieces[mask], 0)
            out.append(whole)
        return out

    def times(self, rows_rel, halves):
        outs = []
        for pieces in halves:
            total = None
            for mask, piece in pieces.items():
                start = self.place(mask) // 4 * piece.shape[0]
                term = dot_f32(rows_rel[:, start : start + piece.shape[0]], piece)
                total = term if total is None else total + term
            outs.append(total)
        return outs

    def times_back(self, parts, halves):
        masks = sorted(halves[0], key=self.place)
        blocks = []
        for mask in masks:
            total = None
            for part, pieces in zip(parts, halves):
                term = dot_rows(part, pieces[mask])
                total = term if total is None else total + term
            blocks.append(total)
        return jnp.concatenate(blocks, axis=1)

    def reduce_scatter(self, rows_rel, grads, split):
        width = rows_rel.shape[1]
        unit = width // self.shards * 4
        outs = []
        for part, flip in ((grads[:, :split], True), (grads[:, split:], False)):
            order = self.near[::-1] if flip else self.near
            masks = [0]
            for bit in reversed(order):
                masks = masks + [m | (1 << bit) for m in masks]
            cols = [
                rows_rel[:, self.place(m) // 4 * unit : (self.place(m) // 4 + 1) * unit]
                for m in masks + [m | 1 for m in masks]
            ]
            quarter = len(cols) // 4
            groups = [jnp.concatenate(cols[g * quarter : (g + 1) * quarter], axis=1) for g in range(4)]
            got_hi = self.swap(dot_tokens(groups[3], part).astype(BF16), 0)
            got_lo = self.swap(dot_tokens(groups[2], part).astype(BF16), 0)
            high = dot_tokens(groups[1], part) + got_hi.astype(F32)
            got = self.swap(high.astype(BF16), order[0])
            total = dot_tokens(groups[0], part) + got_lo.astype(F32) + got.astype(F32)
            for bit in tuple(order[1:]) + self.far[::-1]:
                half = total.shape[0] // 2
                got = self.swap(total[half:].astype(BF16), bit)
                total = total[:half] + got.astype(F32)
            outs.append(total)
        return jnp.concatenate(outs, axis=1)

    def reduce_small(self, terms):
        index = lax.axis_index(AXIS)
        blocks = terms.reshape(self.shards, -1)
        for bit in range(self.bits):
            pairs = blocks.reshape(-1, 2, blocks.shape[-1])
            mine = (index >> bit) & 1
            keep = jnp.where(mine == 1, pairs[:, 1], pairs[:, 0])
            send = jnp.where(mine == 1, pairs[:, 0], pairs[:, 1])
            blocks = keep + self.swap(send, bit)
        return blocks.reshape(terms.shape[0] // self.shards, terms.shape[1])

    def sum_all(self, value):
        for bit in range(self.bits):
            value = value + self.swap(value, bit)
        return value


def xor_blocks(rows, base, order):
    tokens, width = rows.shape
    block = width // len(order)

    def kernel(base_ref, in_ref, out_ref):
        base_value = base_ref[0]
        if block % LANES == 0:
            for j, mask in enumerate(order):
                start = pl.multiple_of((base_value ^ mask) * block, LANES)
                out_ref[:, j * block : (j + 1) * block] = in_ref[:, pl.ds(start, block)]
            return
        per_tile = LANES // block
        lane = lax.broadcasted_iota(jnp.int32, (tokens, LANES), 1) // block
        for tile in range(width // LANES):
            joined = None
            for sub in range(per_tile):
                source = base_value ^ order[tile * per_tile + sub]
                start = pl.multiple_of(source // per_tile * LANES, LANES)
                piece = in_ref[:, pl.ds(start, LANES)].astype(F32)
                shift = (sub + per_tile - source % per_tile) % per_tile * block
                piece = pltpu.roll(piece, shift, 1)
                joined = piece if joined is None else jnp.where(lane == sub, piece, joined)
            out_ref[:, tile * LANES : (tile + 1) * LANES] = joined.astype(out_ref.dtype)

    return pl.pallas_call(
        kernel,
        out_shape=jax.ShapeDtypeStruct(rows.shape, rows.dtype),
        in_specs=[
            pl.BlockSpec(memory_space=pltpu.SMEM),
            pl.BlockSpec(memory_space=pltpu.VMEM),
        ],
        out_specs=pl.BlockSpec(memory_space=pltpu.VMEM),
        name="xor_blocks",
    )(base.astype(jnp.int32).reshape(1), rows)


def after(value, *others):
    return lax.optimization_barrier((value,) + others)[0]


def solution(mesh):
    wires = Wires(mesh.shape[AXIS])

    def local(
        tokens,
        seg_ids,
        routes,
        attn_gain,
        w_query,
        key_projection_weight,
        value_projection_weight,
        w_out,
        query_key_gains,
        ffn_gain,
        w_router,
        w_gate,
        w_up,
        w_down,
        cotangent,
    ):
        token_count, model_width = tokens.shape
        experts = w_router.shape[1]
        head_size = query_key_gains.shape[1]
        query_width, kv_width = w_query.shape[1], key_projection_weight.shape[1]
        query_heads, kv_heads = query_width // head_size, kv_width // head_size
        group = query_heads // kv_heads
        score_scale = 1.0 / math.sqrt(head_size)
        capacity = 5 * token_count * routes.shape[1] // (4 * experts)
        assert w_gate.shape[0] == 1 and experts == wires.shards

        small_rows = w_router.shape[0]
        small = jnp.concatenate(
            [
                w_router,
                attn_gain[:, None],
                ffn_gain[:, None],
                jnp.zeros((small_rows, LANES - (experts + 2) % LANES), BF16),
            ],
            axis=1,
        )
        small_all = wires.gather_small(small)
        router_weight = small_all[:, :experts]
        gain_first = small_all[:, experts].astype(F32)
        gain_second = small_all[:, experts + 1].astype(F32)

        packed = jnp.concatenate([w_query, key_projection_weight, value_projection_weight], axis=1)
        packed_split = packed.shape[1] // 2 // LANES * LANES
        packed_far = wires.gather_far(packed)
        packed_near = wires.gather_near(packed_far, packed_split)
        packed_weight = wires.gather_core(packed_near)
        out_split = model_width // 2
        out_far = wires.gather_far(after(w_out, packed_far))
        out_near = wires.gather_near(
            after(out_far, *[piece for half in packed_near for piece in half.values()]), out_split
        )
        out_weight = wires.gather_core(out_near)

        expert_ids = jnp.arange(experts, dtype=jnp.int32)
        chosen = jnp.any(routes[:, :, None] == expert_ids[None, None, :], axis=1)
        row_index = jnp.arange(token_count, dtype=jnp.int32)
        earlier = (row_index[None, :] < row_index[:, None]).astype(BF16)
        slot = dot_f32(earlier, chosen.astype(BF16)).astype(jnp.int32)
        slot_ids = jnp.arange(capacity, dtype=jnp.int32)
        slot_hot = chosen.T[:, None, :] & (slot.T[:, None, :] == slot_ids[None, :, None])
        slot_pick = slot_hot.astype(BF16)

        def to_experts(rows):
            picked = jnp.einsum("est,td->esd", slot_pick, rows, preferred_element_type=F32)
            return exchange(picked.astype(BF16))

        def exchange(blocks):
            return lax.all_to_all(blocks, AXIS, split_axis=0, concat_axis=0, tiled=True)

        cot_arrived = to_experts(after(cotangent.astype(BF16), packed_far))

        segment = seg_ids[0]
        allowed, cosine_lookup, sine_lookup = layout(segment, head_size)
        tokens_wide = tokens.astype(F32)
        normed_first, unit_first, factor_first = norm_rows(tokens_wide, gain_first)
        rows_rel = wires.to_relative(normed_first.astype(BF16))
        projected = jnp.concatenate(wires.times(rows_rel, packed_weight), axis=1)
        query_proj = projected[:, :query_width].reshape(token_count, query_heads, head_size)
        key_proj = projected[:, query_width : query_width + kv_width].reshape(
            token_count, kv_heads, head_size
        )
        value_proj = (
            projected[:, query_width + kv_width :]
            .astype(BF16)
            .reshape(token_count, kv_heads, head_size)
        )
        query_normed, query_unit, query_factor = norm_rows(query_proj, query_key_gains[0])
        key_normed, key_unit, key_factor = norm_rows(key_proj, query_key_gains[1])
        query_rot = (
            apply_rotary(query_normed, cosine_lookup, sine_lookup)
            .astype(BF16)
            .reshape(token_count, kv_heads, group, head_size)
        )
        key_rot = apply_rotary(key_normed, cosine_lookup, sine_lookup).astype(BF16)
        scores = (
            jnp.einsum("tngd,snd->ngts", query_rot, key_rot, preferred_element_type=F32)
            * score_scale
        )
        masked = jnp.where(allowed, scores, -MASK_FLOOR)
        row_top = jnp.max(masked, axis=-1, keepdims=True)
        weights_raw = jnp.where(allowed, jnp.exp(masked - row_top), 0.0)
        row_total = jnp.sum(weights_raw, axis=-1, keepdims=True)
        log_total = row_top + jnp.log(row_total)
        attn_probs = (weights_raw / row_total).astype(BF16)
        head_out = jnp.einsum(
            "ngts,snd->tngd", attn_probs, value_proj, preferred_element_type=F32
        ).astype(BF16)
        heads_rel = wires.to_relative(head_out.reshape(token_count, query_width))
        residual_mid = tokens_wide + jnp.concatenate(wires.times(heads_rel, out_weight), axis=1)

        normed_second, unit_second, factor_second = norm_rows(residual_mid, gain_second)
        moe_rows = normed_second.astype(BF16)
        logits = dot_f32(moe_rows, router_weight)
        logit_top = jnp.max(jnp.where(chosen, logits, -MASK_FLOOR), axis=-1, keepdims=True)
        share_raw = jnp.where(chosen, jnp.exp(jnp.where(chosen, logits - logit_top, 0.0)), 0.0)
        route_share = share_raw / jnp.sum(share_raw, axis=-1, keepdims=True)
        share_pick = jnp.where(slot_hot, route_share.T[:, None, :], 0.0)
        arrived = to_experts(moe_rows)
        share_arrived = exchange(jnp.sum(share_pick, axis=-1))[:, :, None]
        gate_weight, up_weight, down_weight = w_gate[0], w_up[0], w_down[0]

        def rows_times(pattern, left, right):
            return jnp.einsum(pattern, left, right, preferred_element_type=F32)

        gate_pre = rows_times("scd,df->scf", arrived, gate_weight)
        up_pre = rows_times("scd,df->scf", arrived, up_weight)
        sigmoid_gate = jax.nn.sigmoid(gate_pre)
        silu_gate = gate_pre * sigmoid_gate
        hidden_wide = silu_gate * up_pre
        hidden = hidden_wide.astype(BF16)
        result = rows_times("scf,fd->scd", hidden, down_weight).astype(BF16)
        share_grad_slots = exchange(jnp.sum(cot_arrived.astype(F32) * result.astype(F32), axis=-1))

        grad_hidden = rows_times("scd,fd->scf", cot_arrived, down_weight) * share_arrived
        grad_gate_pre = (
            grad_hidden * up_pre * sigmoid_gate * (1.0 + gate_pre * (1.0 - sigmoid_gate))
        ).astype(BF16)
        grad_up_pre = (grad_hidden * silu_gate).astype(BF16)
        grad_back = (
            rows_times("scf,df->scd", grad_gate_pre, gate_weight)
            + rows_times("scf,df->scd", grad_up_pre, up_weight)
        ).astype(BF16)
        grad_returned = exchange(grad_back)
        shared_hidden = (hidden_wide * share_arrived).astype(BF16)
        grad_down = rows_times("scf,scd->fd", shared_hidden, cot_arrived)
        grad_gate = rows_times("scd,scf->df", arrived, grad_gate_pre)
        grad_up = rows_times("scd,scf->df", arrived, grad_up_pre)

        grad_share = jnp.sum(jnp.where(slot_hot, share_grad_slots[:, :, None], 0.0), axis=1).T
        grad_chosen = route_share * (
            grad_share - jnp.sum(route_share * grad_share, axis=1, keepdims=True)
        )
        grad_logits = grad_chosen.astype(BF16)
        router_term = dot_tokens(moe_rows, grad_logits)
        grad_second = rows_times("est,esd->td", slot_pick, grad_returned) + dot_rows(
            grad_logits, router_weight
        )
        second_gain_term = jnp.sum(grad_second * unit_second, axis=0)
        grad_mid = cotangent + norm_gradient_rows(
            grad_second, unit_second, factor_second, gain_second
        )
        grad_attn = grad_mid.astype(BF16)

        returned = exchange(after(result, grad_returned))
        share_high = share_pick.astype(BF16)
        share_low = (share_pick - share_high.astype(F32)).astype(BF16)
        moe_sum = rows_times("est,esd->td", share_high, returned) + rows_times(
            "est,esd->td", share_low, returned
        )
        block_out = (residual_mid + moe_sum).astype(BF16)

        grad_out = wires.reduce_scatter(heads_rel, grad_attn, out_split)
        grad_parts = (grad_attn[:, :out_split], grad_attn[:, out_split:])
        heads_gradient = wires.to_natural(
            wires.times_back(grad_parts, out_weight).astype(BF16)
        ).reshape(head_out.shape)
        scores_again = (
            jnp.einsum("tngd,snd->ngts", query_rot, key_rot, preferred_element_type=F32)
            * score_scale
        )
        probs_again = jnp.where(
            allowed, jnp.exp(jnp.where(allowed, scores_again, -MASK_FLOOR) - log_total), 0.0
        )
        grad_probs = jnp.einsum(
            "tngd,snd->ngts", heads_gradient, value_proj, preferred_element_type=F32
        )
        row_delta = jnp.einsum(
            "tngd,tngd->ngt", heads_gradient, head_out, preferred_element_type=F32
        )[..., None]
        grad_scores = (probs_again * (grad_probs - row_delta)).astype(BF16)
        grad_qrot = (
            jnp.einsum("ngts,snd->tngd", grad_scores, key_rot, preferred_element_type=F32)
            * score_scale
        ).reshape(token_count, query_heads, head_size)
        grad_krot = (
            jnp.einsum("qwor,oqwk->rqk", grad_scores, query_rot, preferred_element_type=F32)
            * score_scale
        )
        grad_vproj = (
            jnp.einsum(
                "qwor,oqwk->rqk",
                probs_again.astype(BF16),
                heads_gradient,
                preferred_element_type=F32,
            )
            .astype(BF16)
            .reshape(token_count, kv_width)
        )
        query_back = apply_rotary(grad_qrot, cosine_lookup, -sine_lookup)
        key_back = apply_rotary(grad_krot, cosine_lookup, -sine_lookup)
        gain_terms = jnp.stack(
            [
                jnp.sum(query_back * query_unit, axis=(0, 1)),
                jnp.sum(key_back * key_unit, axis=(0, 1)),
            ]
        )
        grad_qk_gains = wires.sum_all(gain_terms)
        query_raw = (
            norm_gradient_rows(query_back, query_unit, query_factor, query_key_gains[0])
            .astype(BF16)
            .reshape(token_count, query_width)
        )
        key_raw = (
            norm_gradient_rows(key_back, key_unit, key_factor, query_key_gains[1])
            .astype(BF16)
            .reshape(token_count, kv_width)
        )
        raw = jnp.concatenate([query_raw, key_raw, grad_vproj], axis=1)
        grad_packed = wires.reduce_scatter(rows_rel, raw, packed_split)
        raw_parts = (raw[:, :packed_split], raw[:, packed_split:])
        grad_normed = wires.to_natural(wires.times_back(raw_parts, packed_weight))
        first_gain_term = jnp.sum(grad_normed * unit_first, axis=0)
        grad_tokens = grad_mid + norm_gradient_rows(
            grad_normed, unit_first, factor_first, gain_first
        )
        small_terms = jnp.concatenate(
            [
                router_term,
                first_gain_term[:, None],
                second_gain_term[:, None],
                jnp.zeros((model_width, LANES - (experts + 2) % LANES), F32),
            ],
            axis=1,
        )
        grad_small = wires.reduce_small(small_terms)
        return (
            block_out,
            grad_tokens,
            grad_small[:, experts],
            grad_packed[:, :query_width],
            grad_packed[:, query_width : query_width + kv_width],
            grad_packed[:, query_width + kv_width :],
            grad_out,
            grad_qk_gains,
            grad_small[:, experts + 1],
            grad_small[:, :experts],
            grad_gate[None],
            grad_up[None],
            grad_down[None],
        )

    rows = P(AXIS, None)
    flat = P(AXIS)
    stack = P(AXIS, None, None)
    return jax.shard_map(
        local,
        mesh=mesh,
        in_specs=(rows, rows, rows, flat, rows, rows, rows, rows, P(), flat, rows)
        + (stack, stack, stack, rows),
        out_specs=(rows, rows, flat, rows, rows, rows, rows, P(), flat, rows, stack, stack, stack),
        check_vma=False,
    )
```

```python
import math

import jax
import jax.numpy as jnp
from jax import lax
from jax.experimental import pallas as pl
from jax.experimental.pallas import tpu as pltpu
from jax.sharding import PartitionSpec as P

NORM_EPSILON = 1e-06
ROPE_THETA = 1000000.0
MASK_FLOOR = 1e30
LANES = 128
AXIS = "expert"
F32 = jnp.float32
BF16 = jnp.bfloat16


def dot_f32(left, right):
    return jnp.dot(left, right, preferred_element_type=F32)


def dot_rows(left, right):
    return jnp.einsum("tj,ij->ti", left, right, preferred_element_type=F32)


def dot_tokens(left, right):
    return jnp.einsum("ti,tj->ij", left, right, preferred_element_type=F32)


def norm_rows(values, gain_vector):
    factor = lax.rsqrt(jnp.mean(values * values, axis=-1, keepdims=True) + NORM_EPSILON)
    unit_rows = values * factor
    return (unit_rows * gain_vector, unit_rows, factor)


def norm_gradient_rows(gradient, unit_rows, factor, gain_vector):
    scaled = gradient * gain_vector
    return factor * (scaled - unit_rows * jnp.mean(scaled * unit_rows, axis=-1, keepdims=True))


def apply_rotary(values, cosine_lookup, sine_lookup):
    half_size = values.shape[-1] // 2
    first_half = values[..., :half_size]
    second_half = values[..., half_size:]
    cos_wide = cosine_lookup[:, None, :]
    sin_wide = sine_lookup[:, None, :]
    return jnp.concatenate(
        [
            first_half * cos_wide - second_half * sin_wide,
            second_half * cos_wide + first_half * sin_wide,
        ],
        axis=-1,
    )


def layout(segment, head_size):
    row_count = segment.shape[0]
    row_index = jnp.arange(row_count, dtype=jnp.int32)
    same_seq = segment[:, None] == segment[None, :]
    positions = jnp.sum(
        jnp.where(same_seq & (row_index[None, :] < row_index[:, None]), 1, 0), axis=1
    ).astype(jnp.int32)
    allowed = same_seq & (row_index[None, :] <= row_index[:, None])
    half_size = head_size // 2
    inverse_freq = ROPE_THETA ** (-jnp.arange(half_size, dtype=F32) / half_size)
    angles = positions.astype(F32)[:, None] * inverse_freq[None, :]
    return (allowed, jnp.cos(angles), jnp.sin(angles))


class Wires:
    def __init__(self, shards):
        self.shards = shards
        self.bits = shards.bit_length() - 1
        assert shards == 1 << self.bits and self.bits >= 3
        self.far = (self.bits - 1, self.bits - 2)
        self.near = tuple(range(1, self.bits - 2))

    def swap(self, block, bit):
        return lax.ppermute(block, AXIS, [(i, i ^ (1 << bit)) for i in range(self.shards)])

    def place(self, mask):
        spot = 0
        for bit in range(self.bits):
            if bit == self.bits - 1:
                to = 0
            elif bit == self.bits - 2:
                to = 1
            elif bit == 0:
                to = self.bits - 1
            else:
                to = bit + 1
            spot = spot | (((mask >> bit) & 1) << to)
        return spot

    def to_relative(self, rows):
        order = [0] * self.shards
        for mask in range(self.shards):
            order[self.place(mask)] = mask
        return xor_blocks(rows, lax.axis_index(AXIS), order)

    def to_natural(self, rows):
        order = [self.place(block) for block in range(self.shards)]
        return xor_blocks(rows, self.place(lax.axis_index(AXIS)), order)

    def gather_small(self, shard):
        for bit in self.far + self.near + (0,):
            shard = jnp.concatenate([shard, self.swap(shard, bit)], axis=0)
        return self.to_natural(shard.T)

    def gather_far(self, shard):
        high, low = self.far
        across = self.swap(shard, high)
        return jnp.concatenate(
            [shard, across, self.swap(shard, low), self.swap(across, low)], axis=0
        )

    def gather_near(self, stacks):
        halves = []
        for part, order in zip(stacks, (self.near, self.near[::-1])):
            pieces = {0: part}
            for bit in order:
                for mask in list(pieces):
                    pieces[mask | (1 << bit)] = self.swap(pieces[mask], bit)
            halves.append(pieces)
        return halves

    def gather_core(self, halves):
        out = []
        for pieces in halves:
            whole = dict(pieces)
            for mask in list(pieces):
                whole[mask | 1] = self.swap(pieces[mask], 0)
            out.append(whole)
        return out

    def times(self, rows_rel, halves):
        outs = []
        for pieces in halves:
            total = None
            for mask, piece in pieces.items():
                start = self.place(mask) // 4 * piece.shape[0]
                term = dot_f32(rows_rel[:, start : start + piece.shape[0]], piece)
                total = term if total is None else total + term
            outs.append(total)
        return outs

    def times_back(self, parts, halves):
        masks = sorted(halves[0], key=self.place)
        blocks = []
        for mask in masks:
            total = None
            for part, pieces in zip(parts, halves):
                term = dot_rows(part, pieces[mask])
                total = term if total is None else total + term
            blocks.append(total)
        return jnp.concatenate(blocks, axis=1)

    def reduce_scatter(self, rows_rel, grads, split):
        width = rows_rel.shape[1]
        unit = width // self.shards * 4
        outs = []
        for part, flip in ((grads[:, :split], True), (grads[:, split:], False)):
            order = self.near[::-1] if flip else self.near
            masks = [0]
            for bit in reversed(order):
                masks = masks + [m | (1 << bit) for m in masks]
            cols = [
                rows_rel[:, self.place(m) // 4 * unit : (self.place(m) // 4 + 1) * unit]
                for m in masks + [m | 1 for m in masks]
            ]
            quarter = len(cols) // 4
            groups = [jnp.concatenate(cols[g * quarter : (g + 1) * quarter], axis=1) for g in range(4)]
            got_hi = self.swap(dot_tokens(groups[3], part).astype(BF16), 0)
            got_lo = self.swap(dot_tokens(groups[2], part).astype(BF16), 0)
            high = dot_tokens(groups[1], part) + got_hi.astype(F32)
            got = self.swap(high.astype(BF16), order[0])
            total = dot_tokens(groups[0], part) + got_lo.astype(F32) + got.astype(F32)
            for bit in tuple(order[1:]) + self.far[::-1]:
                half = total.shape[0] // 2
                got = self.swap(total[half:].astype(BF16), bit)
                total = total[:half] + got.astype(F32)
            outs.append(total)
        return jnp.concatenate(outs, axis=1)


def xor_blocks(rows, base, order):
    tokens, width = rows.shape
    block = width // len(order)

    def kernel(base_ref, in_ref, out_ref):
        base_value = base_ref[0]
        if block % LANES == 0:
            for j, mask in enumerate(order):
                start = pl.multiple_of((base_value ^ mask) * block, LANES)
                out_ref[:, j * block : (j + 1) * block] = in_ref[:, pl.ds(start, block)]
            return
        per_tile = LANES // block
        lane = lax.broadcasted_iota(jnp.int32, (tokens, LANES), 1) // block
        for tile in range(width // LANES):
            joined = None
            for sub in range(per_tile):
                source = base_value ^ order[tile * per_tile + sub]
                start = pl.multiple_of(source // per_tile * LANES, LANES)
                piece = in_ref[:, pl.ds(start, LANES)].astype(F32)
                shift = (sub + per_tile - source % per_tile) % per_tile * block
                piece = pltpu.roll(piece, shift, 1)
                joined = piece if joined is None else jnp.where(lane == sub, piece, joined)
            out_ref[:, tile * LANES : (tile + 1) * LANES] = joined.astype(out_ref.dtype)

    return pl.pallas_call(
        kernel,
        out_shape=jax.ShapeDtypeStruct(rows.shape, rows.dtype),
        in_specs=[
            pl.BlockSpec(memory_space=pltpu.SMEM),
            pl.BlockSpec(memory_space=pltpu.VMEM),
        ],
        out_specs=pl.BlockSpec(memory_space=pltpu.VMEM),
        name="xor_blocks",
    )(base.astype(jnp.int32).reshape(1), rows)


def after(value, *others):
    return lax.optimization_barrier((value,) + others)[0]


def solution(mesh):
    wires = Wires(mesh.shape[AXIS])

    def local(
        tokens,
        seg_ids,
        routes,
        attn_gain,
        w_query,
        key_projection_weight,
        value_projection_weight,
        w_out,
        query_key_gains,
        ffn_gain,
        w_router,
        w_gate,
        w_up,
        w_down,
        cotangent,
    ):
        token_count, model_width = tokens.shape
        experts = w_router.shape[1]
        head_size = query_key_gains.shape[1]
        query_width, kv_width = w_query.shape[1], key_projection_weight.shape[1]
        query_heads, kv_heads = query_width // head_size, kv_width // head_size
        group = query_heads // kv_heads
        score_scale = 1.0 / math.sqrt(head_size)
        capacity = 5 * token_count * routes.shape[1] // (4 * experts)
        assert w_gate.shape[0] == 1 and experts == wires.shards

        first_gain_rows = attn_gain.astype(F32)[:, None]
        packed = jnp.concatenate([w_query, key_projection_weight, value_projection_weight], axis=1)
        packed = (packed.astype(F32) * first_gain_rows).astype(BF16)
        packed_split = packed.shape[1] // 2 // LANES * LANES
        out_split = model_width // 2
        far_left = wires.gather_far(packed[:, :packed_split])
        far_right = wires.gather_far(after(packed[:, packed_split:], far_left))
        packed_near = wires.gather_near((far_left, far_right))
        packed_weight = wires.gather_core(packed_near)
        out_left = wires.gather_far(after(w_out[:, :out_split], far_right))
        out_right = wires.gather_far(after(w_out[:, out_split:], out_left))
        arrivals = [piece for half in packed_near for piece in half.values()]
        out_near = wires.gather_near(
            (after(out_left, *arrivals), after(out_right, *arrivals))
        )
        out_weight = wires.gather_core(out_near)

        pad = LANES - (experts + 2) % LANES
        small = jnp.concatenate(
            [w_router, ffn_gain[:, None], jnp.zeros((w_router.shape[0], pad + 1), BF16)], axis=1
        )
        small_all = wires.gather_small(after(small, out_right))
        router_turned = small_all[:experts]
        gain_second = small_all[experts].astype(F32)

        expert_ids = jnp.arange(experts, dtype=jnp.int32)
        chosen = jnp.any(routes[:, :, None] == expert_ids[None, None, :], axis=1)
        row_index = jnp.arange(token_count, dtype=jnp.int32)
        earlier = (row_index[None, :] < row_index[:, None]).astype(BF16)
        slot = dot_f32(earlier, chosen.astype(BF16)).astype(jnp.int32)
        slot_ids = jnp.arange(capacity, dtype=jnp.int32)
        slot_hot = chosen.T[:, None, :] & (slot.T[:, None, :] == slot_ids[None, :, None])
        slot_pick = slot_hot.astype(BF16)

        def to_experts(rows):
            picked = jnp.einsum("est,td->esd", slot_pick, rows, preferred_element_type=F32)
            return exchange(picked.astype(BF16))

        def exchange(blocks):
            return lax.all_to_all(blocks, AXIS, split_axis=0, concat_axis=0, tiled=True)

        cot_arrived = to_experts(after(cotangent.astype(BF16), far_right))

        segment = seg_ids[0]
        allowed, cosine_lookup, sine_lookup = layout(segment, head_size)
        tokens_wide = tokens.astype(F32)
        unit_first, _, factor_first = norm_rows(tokens_wide, 1.0)
        rows_rel = wires.to_relative(unit_first.astype(BF16))
        projected = jnp.concatenate(wires.times(rows_rel, packed_weight), axis=1)
        query_proj = projected[:, :query_width].reshape(token_count, query_heads, head_size)
        key_proj = projected[:, query_width : query_width + kv_width].reshape(
            token_count, kv_heads, head_size
        )
        value_proj = (
            projected[:, query_width + kv_width :]
            .astype(BF16)
            .reshape(token_count, kv_heads, head_size)
        )
        query_normed, query_unit, query_factor = norm_rows(query_proj, query_key_gains[0])
        key_normed, key_unit, key_factor = norm_rows(key_proj, query_key_gains[1])
        query_rot = (
            apply_rotary(query_normed, cosine_lookup, sine_lookup)
            .astype(BF16)
            .reshape(token_count, kv_heads, group, head_size)
        )
        key_rot = apply_rotary(key_normed, cosine_lookup, sine_lookup).astype(BF16)
        scores = (
            jnp.einsum("tngd,snd->ngts", query_rot, key_rot, preferred_element_type=F32)
            * score_scale
        )
        masked = jnp.where(allowed, scores, -MASK_FLOOR)
        row_top = jnp.max(masked, axis=-1, keepdims=True)
        weights_raw = jnp.where(allowed, jnp.exp(masked - row_top), 0.0)
        row_total = jnp.sum(weights_raw, axis=-1, keepdims=True)
        log_total = row_top + jnp.log(row_total)
        attn_probs = (weights_raw / row_total).astype(BF16)
        head_out = jnp.einsum(
            "ngts,snd->tngd", attn_probs, value_proj, preferred_element_type=F32
        ).astype(BF16)
        heads_rel = wires.to_relative(head_out.reshape(token_count, query_width))
        residual_mid = tokens_wide + jnp.concatenate(wires.times(heads_rel, out_weight), axis=1)

        normed_second, unit_second, factor_second = norm_rows(residual_mid, gain_second)
        moe_rows = normed_second.astype(BF16)
        logits = dot_rows(moe_rows, router_turned)
        logit_top = jnp.max(jnp.where(chosen, logits, -MASK_FLOOR), axis=-1, keepdims=True)
        share_raw = jnp.where(chosen, jnp.exp(jnp.where(chosen, logits - logit_top, 0.0)), 0.0)
        route_share = share_raw / jnp.sum(share_raw, axis=-1, keepdims=True)
        share_pick = jnp.where(slot_hot, route_share.T[:, None, :], 0.0)
        arrived = to_experts(moe_rows)
        share_arrived = exchange(jnp.sum(share_pick, axis=-1))[:, :, None]
        gate_weight, up_weight, down_weight = w_gate[0], w_up[0], w_down[0]

        def rows_times(pattern, left, right):
            return jnp.einsum(pattern, left, right, preferred_element_type=F32)

        gate_pre = rows_times("scd,df->scf", arrived, gate_weight)
        up_pre = rows_times("scd,df->scf", arrived, up_weight)
        sigmoid_gate = jax.nn.sigmoid(gate_pre)
        silu_gate = gate_pre * sigmoid_gate
        hidden_wide = silu_gate * up_pre
        hidden = hidden_wide.astype(BF16)
        result = rows_times("scf,fd->scd", hidden, down_weight).astype(BF16)
        share_grad_slots = exchange(jnp.sum(cot_arrived.astype(F32) * result.astype(F32), axis=-1))

        grad_hidden = rows_times("scd,fd->scf", cot_arrived, down_weight) * share_arrived
        grad_gate_pre = (
            grad_hidden * up_pre * sigmoid_gate * (1.0 + gate_pre * (1.0 - sigmoid_gate))
        ).astype(BF16)
        grad_up_pre = (grad_hidden * silu_gate).astype(BF16)
        grad_back = (
            rows_times("scf,df->scd", grad_gate_pre, gate_weight)
            + rows_times("scf,df->scd", grad_up_pre, up_weight)
        ).astype(BF16)
        grad_returned = exchange(grad_back)
        shared_hidden = (hidden_wide * share_arrived).astype(BF16)
        grad_down = rows_times("scf,scd->fd", shared_hidden, cot_arrived)
        grad_gate = rows_times("scd,scf->df", arrived, grad_gate_pre)
        grad_up = rows_times("scd,scf->df", arrived, grad_up_pre)

        grad_share = jnp.sum(jnp.where(slot_hot, share_grad_slots[:, :, None], 0.0), axis=1).T
        grad_chosen = route_share * (
            grad_share - jnp.sum(route_share * grad_share, axis=1, keepdims=True)
        )
        grad_logits = grad_chosen.astype(BF16)
        router_term = dot_tokens(moe_rows, grad_logits)
        grad_second = rows_times("est,esd->td", slot_pick, grad_returned) + dot_f32(
            grad_logits, router_turned
        )
        second_gain_term = jnp.sum(grad_second * unit_second, axis=0)
        grad_mid = cotangent + norm_gradient_rows(
            grad_second, unit_second, factor_second, gain_second
        )
        grad_attn = grad_mid.astype(BF16)

        returned = exchange(after(result, grad_returned))
        share_high = share_pick.astype(BF16)
        share_low = (share_pick - share_high.astype(F32)).astype(BF16)
        moe_sum = rows_times("est,esd->td", share_high, returned) + rows_times(
            "est,esd->td", share_low, returned
        )
        block_out = (residual_mid + moe_sum).astype(BF16)

        grad_out = wires.reduce_scatter(heads_rel, grad_attn, out_split)
        grad_parts = (grad_attn[:, :out_split], grad_attn[:, out_split:])
        heads_gradient = wires.to_natural(
            wires.times_back(grad_parts, out_weight).astype(BF16)
        ).reshape(head_out.shape)
        scores_again = (
            jnp.einsum("tngd,snd->ngts", query_rot, key_rot, preferred_element_type=F32)
            * score_scale
        )
        probs_again = jnp.where(
            allowed, jnp.exp(jnp.where(allowed, scores_again, -MASK_FLOOR) - log_total), 0.0
        )
        grad_probs = jnp.einsum(
            "tngd,snd->ngts", heads_gradient, value_proj, preferred_element_type=F32
        )
        row_delta = jnp.einsum(
            "tngd,tngd->ngt", heads_gradient, head_out, preferred_element_type=F32
        )[..., None]
        grad_scores = (probs_again * (grad_probs - row_delta)).astype(BF16)
        grad_qrot = (
            jnp.einsum("ngts,snd->tngd", grad_scores, key_rot, preferred_element_type=F32)
            * score_scale
        ).reshape(token_count, query_heads, head_size)
        grad_krot = (
            jnp.einsum("qwor,oqwk->rqk", grad_scores, query_rot, preferred_element_type=F32)
            * score_scale
        )
        grad_vproj = (
            jnp.einsum(
                "qwor,oqwk->rqk",
                probs_again.astype(BF16),
                heads_gradient,
                preferred_element_type=F32,
            )
            .astype(BF16)
            .reshape(token_count, kv_width)
        )
        query_back = apply_rotary(grad_qrot, cosine_lookup, -sine_lookup)
        key_back = apply_rotary(grad_krot, cosine_lookup, -sine_lookup)
        gain_terms = jnp.stack(
            [
                jnp.sum(query_back * query_unit, axis=(0, 1)),
                jnp.sum(key_back * key_unit, axis=(0, 1)),
            ]
        )
        query_raw = (
            norm_gradient_rows(query_back, query_unit, query_factor, query_key_gains[0])
            .astype(BF16)
            .reshape(token_count, query_width)
        )
        key_raw = (
            norm_gradient_rows(key_back, key_unit, key_factor, query_key_gains[1])
            .astype(BF16)
            .reshape(token_count, kv_width)
        )
        raw = jnp.concatenate([query_raw, key_raw, grad_vproj], axis=1)
        grad_packed = wires.reduce_scatter(rows_rel, raw, packed_split)
        raw_parts = (raw[:, :packed_split], raw[:, packed_split:])
        scaled = wires.to_natural(wires.times_back(raw_parts, packed_weight))
        aligned = scaled * unit_first
        first_gain_term = jnp.sum(aligned, axis=0)
        grad_tokens = grad_mid + factor_first * (
            scaled - unit_first * jnp.mean(aligned, axis=-1, keepdims=True)
        )

        small_rows = small.shape[0]
        small_terms = jnp.concatenate(
            [
                router_term,
                first_gain_term[:, None],
                second_gain_term[:, None],
                jnp.zeros((model_width, pad), F32),
            ],
            axis=1,
        ).reshape(wires.shards, small_rows, -1)
        gain_block = jnp.pad(gain_terms, ((0, 6), (0, small_terms.shape[2] - head_size)))
        small_terms = jnp.concatenate(
            [small_terms, jnp.broadcast_to(gain_block, (wires.shards,) + gain_block.shape)], axis=1
        )
        small_sums = lax.psum_scatter(
            small_terms.reshape(-1, small_terms.shape[2]), AXIS, scatter_dimension=0, tiled=True
        )
        grad_small = small_sums[:small_rows]
        grad_qk_gains = small_sums[small_rows : small_rows + 2, :head_size]
        grad_packed = grad_packed * first_gain_rows
        return (
            block_out,
            grad_tokens,
            grad_small[:, experts] / first_gain_rows[:, 0],
            grad_packed[:, :query_width],
            grad_packed[:, query_width : query_width + kv_width],
            grad_packed[:, query_width + kv_width :],
            grad_out,
            grad_qk_gains,
            grad_small[:, experts + 1],
            grad_small[:, :experts],
            grad_gate[None],
            grad_up[None],
            grad_down[None],
        )

    rows = P(AXIS, None)
    flat = P(AXIS)
    stack = P(AXIS, None, None)
    return jax.shard_map(
        local,
        mesh=mesh,
        in_specs=(rows, rows, rows, flat, rows, rows, rows, rows, P(), flat, rows)
        + (stack, stack, stack, rows),
        out_specs=(rows, rows, flat, rows, rows, rows, rows, P(), flat, rows, stack, stack, stack),
        check_vma=False,
    )
```
